32 devices in a mesh: groups: 2 (over x), grid: 8 (over z, y), dp: 2 (over core).
Axes of the slice: x: 2, y: 2, z: 4, core: 2. Of those that a mesh axis runs over, the one named last changes fastest.
Arguments:
- acts: bfloat16 [4, 8, 192, 2560], P(('groups', 'dp'), 'grid'), parts along dimension 0, may hold values from -6 to 6
- cotangent: bfloat16 [4, 8, 192, 2560], P(('groups', 'dp'), 'grid'), parts along dimension 0, may hold values from -1.5 to 1.5
- w_gate: bfloat16 [8, 2560, 1792], P('grid'), may hold values from -0.078125 to 0.078125
- w_up: bfloat16 [8, 2560, 1792], P('grid'), may hold values from -0.078125 to 0.078125
- w_down: bfloat16 [8, 1792, 2560], P('grid'), may hold values from -0.0625 to 0.0625
Outputs:
- block_out: bfloat16 [4, 8, 192, 2560], P(('groups', 'dp'), 'grid'), parts along dimension 0
- input_grad: bfloat16 [4, 8, 192, 2560], P(('groups', 'dp'), 'grid'), parts along dimension 0
- gate_grad: bfloat16 [16, 2560, 1792], P(('groups', 'grid')), parts along dimension 0
- up_grad: bfloat16 [16, 2560, 1792], P(('groups', 'grid')), parts along dimension 0
- down_grad: bfloat16 [16, 1792, 2560], P(('groups', 'grid')), parts along dimension 0
The draws below stay inside these ranges and needn't reach their ends.
There are 2 independent parts, one for each index of `groups`. The reference program is written for one: setup_inputs(seed, part) draws one part's arguments, and reference() takes and returns one part's arrays. A program takes and returns all parts, laid end to end along the dimension named above; an argument that names none is the same for every part. Nothing has to cross between parts.
All inputs are finite; a program needn't handle non-finite values.
Results may differ from the reference program's by a relative error of at most 0.015.
Values may be sent and summed in bfloat16 or wider, within the bound.
A program may use at most 192 MiB of HBM per device.

```python
import jax
import jax.numpy as jnp

D = 5120
FFW = 7168
TOK = 768
GC = 4
GR = 2
N_GRID = 8
N_DP = 2


def block_scale(own_key, shape, pieces, smallest, high):
    def one(dim, shards_of):
        heights = jax.random.uniform(jax.random.fold_in(jax.random.fold_in(own_key, 6), dim), (shards_of,), jnp.float32, smallest / len(pieces), high / len(pieces))
        return jnp.repeat(jnp.exp(heights), shape[dim] // shards_of).reshape((-1,) + (1,) * (len(shape) - dim - 1))

    level = one(*pieces[0])
    for cut in pieces[1:]:
        level = level * one(*cut)
    return level


def normal_values(key, extent, spread, limit, split=(), kind=jnp.bfloat16):
    entries = spread * jax.random.normal(key, extent, jnp.float32)
    if split:
        entries = entries * block_scale(key, extent, split, -0.22, 0.18)
    return jnp.clip(entries, -limit, limit).astype(kind)


def setup_inputs(seed: int = 0, part: int = 0) -> dict:
    key_of = jax.random.split(jax.random.key(seed), 6)
    part_keys = jax.random.split(jax.random.fold_in(key_of[5], part), 6)
    return {
        "acts": normal_values(part_keys[0], (N_DP, N_GRID, TOK // GC, D // GR), 1.0, 6.0, ((0, 2), (1, 8))),
        "cotangent": normal_values(part_keys[1], (N_DP, N_GRID, TOK // GC, D // GR), 0.25, 1.5, ((0, 2), (1, 8))),
        "w_gate": normal_values(key_of[2], (N_GRID, D // GR, FFW // GC), D ** -0.5, 0.078125, ((0, 8),)),
        "w_up": normal_values(key_of[3], (N_GRID, D // GR, FFW // GC), D ** -0.5, 0.078125, ((0, 8),)),
        "w_down": normal_values(key_of[4], (N_GRID, FFW // GC, D // GR), FFW ** -0.5, 0.0625, ((0, 8),)),
    }


def to_rows(tiles):
    blocks = tiles.reshape(N_DP, GR, GC, TOK // GC, D // GR)
    return blocks.transpose(0, 2, 3, 1, 4).reshape(N_DP * TOK, D)


def to_tiles(rows_all):
    blocks = rows_all.reshape(N_DP, GC, TOK // GC, GR, D // GR)
    return blocks.transpose(0, 3, 1, 2, 4).reshape(N_DP, GR * GC, TOK // GC, D // GR)


def weight_rows(tiles):
    return tiles.reshape(GR, GC, D // GR, FFW // GC).transpose(0, 2, 1, 3).reshape(D, FFW)


def weight_tiles(full):
    return full.reshape(GR, D // GR, GC, FFW // GC).transpose(0, 2, 1, 3).reshape(GR * GC, D // GR, FFW // GC)


def down_rows(tiles):
    return tiles.reshape(GR, GC, FFW // GC, D // GR).transpose(1, 2, 0, 3).reshape(FFW, D)


def down_tiles(full):
    return full.reshape(GC, FFW // GC, GR, D // GR).transpose(2, 0, 1, 3).reshape(GR * GC, FFW // GC, D // GR)


def reference(acts, cotangent, w_gate, w_up, w_down):
    inputs = to_rows(acts)
    out_grads = to_rows(cotangent)
    gate_full = weight_rows(w_gate)
    up_full = weight_rows(w_up)
    down_full = down_rows(w_down)
    gate_pre = jnp.dot(inputs, gate_full, preferred_element_type=jnp.float32)
    up_proj = jnp.dot(inputs, up_full, preferred_element_type=jnp.float32)
    sigmoid_g = jax.nn.sigmoid(gate_pre)
    activated = gate_pre * sigmoid_g
    hidden = (activated * up_proj).astype(jnp.bfloat16)
    block_out = (inputs.astype(jnp.float32) + jnp.dot(hidden, down_full, preferred_element_type=jnp.float32)).astype(jnp.bfloat16)
    hidden_grad = jnp.dot(out_grads, down_full.T, preferred_element_type=jnp.float32)
    gate_back = (hidden_grad * up_proj * sigmoid_g * (1.0 + gate_pre * (1.0 - sigmoid_g))).astype(jnp.bfloat16)
    up_back = (hidden_grad * activated).astype(jnp.bfloat16)
    input_sum = jnp.dot(gate_back, gate_full.T, preferred_element_type=jnp.float32) + jnp.dot(up_back, up_full.T, preferred_element_type=jnp.float32)
    input_grad = (out_grads.astype(jnp.float32) + input_sum).astype(jnp.bfloat16)
    gate_grad = jnp.dot(inputs.T, gate_back, preferred_element_type=jnp.float32).astype(jnp.bfloat16)
    up_grad = jnp.dot(inputs.T, up_back, preferred_element_type=jnp.float32).astype(jnp.bfloat16)
    down_grad = jnp.dot(hidden.T, out_grads, preferred_element_type=jnp.float32).astype(jnp.bfloat16)
    return (to_tiles(block_out), to_tiles(input_grad), weight_tiles(gate_grad), weight_tiles(up_grad), down_tiles(down_grad))
```

```python
import jax
import jax.numpy as jnp
from jax import lax
from jax.sharding import PartitionSpec as P


def from_partner(block, axis, stride):
    count = lax.axis_size(axis)
    route = []
    for low in range(count):
        high = low | 1 << stride
        if high != low and high < count:
            route += [(low, high), (high, low)]
    return lax.ppermute(block, axis, route)


def contract_rows(left, right):
    return lax.dot_general(
        left, right, (((0,), (0,)), ((), ())), preferred_element_type=jnp.float32
    )


def contract_cols(left, right):
    return lax.dot_general(
        left, right, (((1,), (1,)), ((), ())), preferred_element_type=jnp.float32
    )


def order_pair(is_upper, mine, other):
    return jnp.where(is_upper, jnp.concatenate([other, mine], 1), jnp.concatenate([mine, other], 1))


def column_sum(partial_term, total_rows, col_bits, row_bits, my_row):
    result_sum = partial_term(0, total_rows)
    for level_bit in range(row_bits - 1, -1, -1):
        half_rows = result_sum.shape[1] // 2
        lower_half = result_sum[:, :half_rows]
        upper_half = result_sum[:, half_rows:]
        is_upper = my_row >> level_bit & 1 == 1
        kept_half = jnp.where(is_upper, upper_half, lower_half)
        given_half = jnp.where(is_upper, lower_half, upper_half)
        result_sum = kept_half + from_partner(
            given_half.astype(jnp.bfloat16), "grid", col_bits + level_bit
        ).astype(given_half.dtype)
    return result_sum


def column_gather(pieces, col_bits, row_bits, my_row):
    for level_bit in range(row_bits):
        partner = from_partner(pieces, "grid", col_bits + level_bit)
        pieces = order_pair(my_row >> level_bit & 1 == 1, pieces, partner)
    return pieces


def row_sum(full_sum, col_bits, my_col):
    for level_bit in range(col_bits - 1, -1, -1):
        half_rows = full_sum.shape[0] // 2
        lower_half = full_sum[:half_rows]
        upper_half = full_sum[half_rows:]
        is_upper = my_col >> level_bit & 1 == 1
        kept_half = jnp.where(is_upper, upper_half, lower_half)
        given_half = jnp.where(is_upper, lower_half, upper_half)
        full_sum = kept_half + from_partner(
            given_half.astype(jnp.bfloat16), "grid", level_bit
        ).astype(given_half.dtype)
    return full_sum


def per_device(acts, cotangent, w_gate, w_up, w_down):
    grid_size = lax.axis_size("grid")
    grid_cols = min(8, grid_size // 2)
    grid_rows = grid_size // grid_cols
    col_bits = grid_cols.bit_length() - 1
    row_bits = grid_rows.bit_length() - 1
    position = lax.axis_index("grid")
    my_row = position // grid_cols
    my_col = position % grid_cols
    own_acts = acts[0, 0]
    own_grads = cotangent[0, 0]
    gate_tile = w_gate[0]
    up_tile = w_up[0]
    down_tile = w_down[0]
    gathered = jnp.stack([own_acts, own_grads])
    for level_bit in range(col_bits):
        partner = from_partner(gathered, "grid", level_bit)
        gathered = order_pair(my_col >> level_bit & 1 == 1, gathered, partner)
    inputs_row = gathered[0]
    out_grad_row = gathered[1]
    total_rows = inputs_row.shape[0]

    def gate_up_term(row_start, row_count):
        return jnp.stack(
            [
                jnp.dot(inputs_row, gate_tile, preferred_element_type=jnp.float32),
                jnp.dot(inputs_row, up_tile, preferred_element_type=jnp.float32),
            ]
        )

    summed = column_sum(gate_up_term, total_rows, col_bits, row_bits, my_row)
    gate_pre = summed[0]
    up_proj = summed[1]
    sigmoid_g = jax.nn.sigmoid(gate_pre)
    activated = gate_pre * sigmoid_g
    hidden = (activated * up_proj).astype(jnp.bfloat16)
    hidden_full = column_gather(hidden[None], col_bits, row_bits, my_row)[0]
    output_sum = row_sum(
        jnp.dot(hidden_full, down_tile, preferred_element_type=jnp.float32), col_bits, my_col
    )
    block_out = (own_acts.astype(jnp.float32) + output_sum).astype(jnp.bfloat16)

    def hidden_grad_term(row_start, row_count):
        return contract_cols(out_grad_row, down_tile)[None]

    hidden_grad = column_sum(hidden_grad_term, total_rows, col_bits, row_bits, my_row)[0]
    gate_back = (hidden_grad * up_proj * sigmoid_g * (1.0 + gate_pre * (1.0 - sigmoid_g))).astype(
        jnp.bfloat16
    )
    up_back = (hidden_grad * activated).astype(jnp.bfloat16)
    backs_full = column_gather(jnp.stack([gate_back, up_back]), col_bits, row_bits, my_row)
    down_local = contract_rows(hidden_full, out_grad_row)
    input_part = contract_cols(backs_full[0], gate_tile) + contract_cols(backs_full[1], up_tile)
    input_sum = row_sum(input_part, col_bits, my_col)
    input_grad = (own_grads.astype(jnp.float32) + input_sum).astype(jnp.bfloat16)
    gate_local = contract_rows(inputs_row, backs_full[0])
    up_local = contract_rows(inputs_row, backs_full[1])
    gate_total, up_total, down_total = (
        lax.psum(gate_local.astype(jnp.bfloat16), "dp").astype(jnp.float32),
        lax.psum(up_local.astype(jnp.bfloat16), "dp").astype(jnp.float32),
        lax.psum(down_local.astype(jnp.bfloat16), "dp").astype(jnp.float32),
    )
    return (
        block_out[None, None],
        input_grad[None, None],
        gate_total.astype(jnp.bfloat16)[None],
        up_total.astype(jnp.bfloat16)[None],
        down_total.astype(jnp.bfloat16)[None],
    )


def flip_grid(block, mask):
    count = lax.axis_size("grid")
    return lax.ppermute(block, "grid", [(i, i ^ mask) for i in range(count)])


def flip_dp(block):
    return lax.ppermute(block, "dp", [(0, 1), (1, 0)])


def after(value, *others):
    return lax.optimization_barrier((value,) + others)[0]


def two_row_device(acts, cotangent, w_gate, w_up, w_down):
    own_acts = acts[0, 0]
    own_grads = cotangent[0, 0]
    gate_tile = w_gate[0]
    up_tile = w_up[0]
    down_tile = w_down[0]
    half = own_acts.shape[0] // 2
    is_upper = lax.axis_index("dp") == 1
    across = 4

    def partial_terms(pair):
        return jnp.stack(
            [
                jnp.dot(pair[0], gate_tile, preferred_element_type=jnp.float32).astype(jnp.bfloat16),
                jnp.dot(pair[0], up_tile, preferred_element_type=jnp.float32).astype(jnp.bfloat16),
                contract_cols(pair[1], down_tile).astype(jnp.bfloat16),
            ]
        )

    def hidden_units(mine, other):
        gate_pre, up_proj, hidden_grad = mine.astype(jnp.float32) + other.astype(jnp.float32)
        sigmoid_g = jax.nn.sigmoid(gate_pre)
        activated = gate_pre * sigmoid_g
        gate_back = hidden_grad * up_proj * sigmoid_g * (1.0 + gate_pre * (1.0 - sigmoid_g))
        return jnp.stack([activated * up_proj, gate_back, hidden_grad * activated]).astype(
            jnp.bfloat16
        )

    def products(units):
        out_part = jnp.dot(units[0], down_tile, preferred_element_type=jnp.float32)
        input_part = contract_cols(units[1], gate_tile) + contract_cols(units[2], up_tile)
        return out_part, input_part

    def weight_grads(pair, pair_dp, units, units_dp, held):
        pairs = order_pair(is_upper, pair, pair_dp)
        all_units = order_pair(is_upper, units, units_dp)
        terms = (
            contract_rows(pairs[0], all_units[1]),
            contract_rows(pairs[0], all_units[2]),
            contract_rows(all_units[0], pairs[1]),
        )
        if held is not None:
            terms = tuple(t + h.astype(jnp.float32) for t, h in zip(terms, held))
        return tuple(t.astype(jnp.bfloat16) for t in terms)

    own = jnp.stack([own_acts, own_grads])
    near = flip_grid(own, 1)
    first, last = own[:, :half], own[:, half:]
    terms_a = partial_terms((own_acts[:half], own_grads[:half]))
    got_a = flip_grid(terms_a, across)
    far = flip_grid(after(own, terms_a), 2)
    own_dp = flip_dp(own)

    terms_1 = partial_terms(near)
    got_1 = flip_grid(terms_1, across)
    near_dp = flip_dp(near)
    corner = flip_grid(far, 1)
    far_dp = flip_dp(far)
    terms_3 = partial_terms(after(corner, terms_1))
    got_3 = flip_grid(terms_3, across)
    corner_dp = flip_dp(corner)
    terms_2 = partial_terms(after(far, terms_3))
    got_2 = flip_grid(terms_2, across)
    terms_b = partial_terms(after(last, terms_2))
    got_b = flip_grid(terms_b, across)

    units_a = hidden_units(terms_a, got_a)
    units_a_dp = flip_dp(units_a)
    out_a, input_a = products(units_a)
    held = weight_grads(first, own_dp[:, :half], units_a, units_a_dp, None)
    held = lax.optimization_barrier(held)

    units_1 = hidden_units(terms_1, got_1)
    units_1_dp = flip_dp(units_1)
    from_near = flip_grid(jnp.stack(products(units_1)).astype(jnp.bfloat16), 1)
    held = weight_grads(near, near_dp, units_1, units_1_dp, held)
    held = lax.optimization_barrier(held)

    units_3 = hidden_units(terms_3, got_3)
    units_3_dp = flip_dp(units_3)
    from_side = flip_grid(jnp.stack(products(units_3)).astype(jnp.bfloat16), 1)
    held = weight_grads(corner, corner_dp, units_3, units_3_dp, held)
    held = lax.optimization_barrier(held)

    units_2 = hidden_units(terms_2, got_2)
    units_2_dp = flip_dp(units_2)
    for_far = jnp.stack(products(units_2)) + from_side.astype(jnp.float32)
    from_far = flip_grid(for_far.astype(jnp.bfloat16), 2)
    held = weight_grads(far, far_dp, units_2, units_2_dp, held)
    held = lax.optimization_barrier(held)

    units_b = hidden_units(terms_b, got_b)
    units_b_dp = flip_dp(units_b)
    out_b, input_b = products(units_b)
    gate_grad, up_grad, down_grad = weight_grads(last, own_dp[:, half:], units_b, units_b_dp, held)

    others = from_near.astype(jnp.float32) + from_far.astype(jnp.float32)
    block_out = own_acts.astype(jnp.float32) + (jnp.concatenate([out_a, out_b]) + others[0])
    input_grad = own_grads.astype(jnp.float32) + (jnp.concatenate([input_a, input_b]) + others[1])
    return (
        block_out.astype(jnp.bfloat16)[None, None],
        input_grad.astype(jnp.bfloat16)[None, None],
        gate_grad[None],
        up_grad[None],
        down_grad[None],
    )


def solution(mesh):
    plan = two_row_device if mesh.shape["grid"] == 8 and mesh.shape["dp"] == 2 else per_device
    return jax.shard_map(
        plan,
        mesh=mesh,
        in_specs=(
            P(("groups", "dp"), "grid", None, None),
            P(("groups", "dp"), "grid", None, None),
            P("grid", None, None),
            P("grid", None, None),
            P("grid", None, None),
        ),
        out_specs=(
            P(("groups", "dp"), "grid", None, None),
            P(("groups", "dp"), "grid", None, None),
            P(("groups", "grid"), None, None),
            P(("groups", "grid"), None, None),
            P(("groups", "grid"), None, None),
        ),
        check_vma=False,
    )
```

```python
import jax
import jax.numpy as jnp
from jax import lax
from jax.sharding import PartitionSpec as P


def from_partner(block, axis, stride):
    count = lax.axis_size(axis)
    route = []
    for low in range(count):
        high = low | 1 << stride
        if high != low and high < count:
            route += [(low, high), (high, low)]
    return lax.ppermute(block, axis, route)


def contract_rows(left, right):
    return lax.dot_general(
        left, right, (((0,), (0,)), ((), ())), preferred_element_type=jnp.float32
    )


def contract_cols(left, right):
    return lax.dot_general(
        left, right, (((1,), (1,)), ((), ())), preferred_element_type=jnp.float32
    )


def order_pair(is_upper, mine, other):
    return jnp.where(is_upper, jnp.concatenate([other, mine], 1), jnp.concatenate([mine, other], 1))


def column_sum(partial_term, total_rows, col_bits, row_bits, my_row):
    result_sum = partial_term(0, total_rows)
    for level_bit in range(row_bits - 1, -1, -1):
        half_rows = result_sum.shape[1] // 2
        lower_half = result_sum[:, :half_rows]
        upper_half = result_sum[:, half_rows:]
        is_upper = my_row >> level_bit & 1 == 1
        kept_half = jnp.where(is_upper, upper_half, lower_half)
        given_half = jnp.where(is_upper, lower_half, upper_half)
        result_sum = kept_half + from_partner(
            given_half.astype(jnp.bfloat16), "grid", col_bits + level_bit
        ).astype(given_half.dtype)
    return result_sum


def column_gather(pieces, col_bits, row_bits, my_row):
    for level_bit in range(row_bits):
        partner = from_partner(pieces, "grid", col_bits + level_bit)
        pieces = order_pair(my_row >> level_bit & 1 == 1, pieces, partner)
    return pieces


def row_sum(full_sum, col_bits, my_col):
    for level_bit in range(col_bits - 1, -1, -1):
        half_rows = full_sum.shape[0] // 2
        lower_half = full_sum[:half_rows]
        upper_half = full_sum[half_rows:]
        is_upper = my_col >> level_bit & 1 == 1
        kept_half = jnp.where(is_upper, upper_half, lower_half)
        given_half = jnp.where(is_upper, lower_half, upper_half)
        full_sum = kept_half + from_partner(
            given_half.astype(jnp.bfloat16), "grid", level_bit
        ).astype(given_half.dtype)
    return full_sum


def per_device(acts, cotangent, w_gate, w_up, w_down):
    grid_size = lax.axis_size("grid")
    grid_cols = min(8, grid_size // 2)
    grid_rows = grid_size // grid_cols
    col_bits = grid_cols.bit_length() - 1
    row_bits = grid_rows.bit_length() - 1
    position = lax.axis_index("grid")
    my_row = position // grid_cols
    my_col = position % grid_cols
    own_acts = acts[0, 0]
    own_grads = cotangent[0, 0]
    gate_tile = w_gate[0]
    up_tile = w_up[0]
    down_tile = w_down[0]
    gathered = jnp.stack([own_acts, own_grads])
    for level_bit in range(col_bits):
        partner = from_partner(gathered, "grid", level_bit)
        gathered = order_pair(my_col >> level_bit & 1 == 1, gathered, partner)
    inputs_row = gathered[0]
    out_grad_row = gathered[1]
    total_rows = inputs_row.shape[0]

    def gate_up_term(row_start, row_count):
        return jnp.stack(
            [
                jnp.dot(inputs_row, gate_tile, preferred_element_type=jnp.float32),
                jnp.dot(inputs_row, up_tile, preferred_element_type=jnp.float32),
            ]
        )

    summed = column_sum(gate_up_term, total_rows, col_bits, row_bits, my_row)
    gate_pre = summed[0]
    up_proj = summed[1]
    sigmoid_g = jax.nn.sigmoid(gate_pre)
    activated = gate_pre * sigmoid_g
    hidden = (activated * up_proj).astype(jnp.bfloat16)
    hidden_full = column_gather(hidden[None], col_bits, row_bits, my_row)[0]
    output_sum = row_sum(
        jnp.dot(hidden_full, down_tile, preferred_element_type=jnp.float32), col_bits, my_col
    )
    block_out = (own_acts.astype(jnp.float32) + output_sum).astype(jnp.bfloat16)

    def hidden_grad_term(row_start, row_count):
        return contract_cols(out_grad_row, down_tile)[None]

    hidden_grad = column_sum(hidden_grad_term, total_rows, col_bits, row_bits, my_row)[0]
    gate_back = (hidden_grad * up_proj * sigmoid_g * (1.0 + gate_pre * (1.0 - sigmoid_g))).astype(
        jnp.bfloat16
    )
    up_back = (hidden_grad * activated).astype(jnp.bfloat16)
    backs_full = column_gather(jnp.stack([gate_back, up_back]), col_bits, row_bits, my_row)
    down_local = contract_rows(hidden_full, out_grad_row)
    input_part = contract_cols(backs_full[0], gate_tile) + contract_cols(backs_full[1], up_tile)
    input_sum = row_sum(input_part, col_bits, my_col)
    input_grad = (own_grads.astype(jnp.float32) + input_sum).astype(jnp.bfloat16)
    gate_local = contract_rows(inputs_row, backs_full[0])
    up_local = contract_rows(inputs_row, backs_full[1])
    gate_total, up_total, down_total = (
        lax.psum(gate_local.astype(jnp.bfloat16), "dp").astype(jnp.float32),
        lax.psum(up_local.astype(jnp.bfloat16), "dp").astype(jnp.float32),
        lax.psum(down_local.astype(jnp.bfloat16), "dp").astype(jnp.float32),
    )
    return (
        block_out[None, None],
        input_grad[None, None],
        gate_total.astype(jnp.bfloat16)[None],
        up_total.astype(jnp.bfloat16)[None],
        down_total.astype(jnp.bfloat16)[None],
    )


def flip_grid(block, mask):
    count = lax.axis_size("grid")
    return lax.ppermute(block, "grid", [(i, i ^ mask) for i in range(count)])


def flip_dp(block):
    return lax.ppermute(block, "dp", [(0, 1), (1, 0)])


def after(value, *others):
    return lax.optimization_barrier((value,) + others)[0]


def two_row_device(acts, cotangent, w_gate, w_up, w_down):
    return two_row_body(acts[0, 0], cotangent[0, 0], w_gate[0], w_up[0], w_down[0])


def two_row_body(own_acts, own_grads, gate_tile, up_tile, down_tile):
    half = own_acts.shape[0] // 2
    is_upper = lax.axis_index("dp") == 1
    across = 4

    def each(move, pair, *mask):
        return tuple(move(x, *mask) for x in pair)

    def to_bf16(value):
        return value.astype(jnp.bfloat16)

    def partial_terms(pair):
        return (
            to_bf16(jnp.dot(pair[0], gate_tile, preferred_element_type=jnp.float32)),
            to_bf16(jnp.dot(pair[0], up_tile, preferred_element_type=jnp.float32)),
            to_bf16(contract_cols(pair[1], down_tile)),
        )

    def exchange(terms):
        return flip_grid(jnp.stack(terms), across)

    def summed(mine, other):
        return [m.astype(jnp.float32) + other[i].astype(jnp.float32) for i, m in enumerate(mine)]

    def gate_values(gate_pre):
        sigmoid_g = jax.nn.sigmoid(gate_pre)
        return sigmoid_g, gate_pre * sigmoid_g

    def hidden_of(gate_pre, up_proj):
        return to_bf16(gate_values(gate_pre)[1] * up_proj)

    def backs_of(gate_pre, up_proj, hidden_grad):
        sigmoid_g, activated = gate_values(gate_pre)
        gate_back = hidden_grad * up_proj * sigmoid_g * (1.0 + gate_pre * (1.0 - sigmoid_g))
        return to_bf16(gate_back), to_bf16(hidden_grad * activated)

    def out_product(hidden):
        return jnp.dot(hidden, down_tile, preferred_element_type=jnp.float32)

    def input_product(backs):
        return contract_cols(backs[0], gate_tile) + contract_cols(backs[1], up_tile)

    def ordered(mine, other):
        return jnp.concatenate(
            [jnp.where(is_upper, other, mine), jnp.where(is_upper, mine, other)]
        )

    def grad_term(left, right, held):
        term = contract_rows(left, right)
        if held is not None:
            term = term + held.astype(jnp.float32)
        return to_bf16(term)

    def finish(mine, other, pair, pair_dp, held):
        values = summed(mine, other)
        hidden = hidden_of(values[0], values[1])
        backs = backs_of(*values)
        units = jnp.stack((hidden,) + backs)
        units_dp = flip_dp(units)
        parts = jnp.stack([out_product(hidden), input_product(backs)])
        left = ordered(pair[0], pair_dp[0])
        right = ordered(pair[1], pair_dp[1])
        all_units = [ordered(units[i], units_dp[i]) for i in range(3)]
        held = held or (None, None, None)
        grads = (
            grad_term(left, all_units[1], held[0]),
            grad_term(left, all_units[2], held[1]),
            grad_term(all_units[0], right, held[2]),
        )
        return parts, lax.optimization_barrier(grads)

    own = (own_acts, own_grads)
    near = each(flip_grid, own, 1)
    first = (own_acts[:half], own_grads[:half])
    last = (own_acts[half:], own_grads[half:])
    terms_a = partial_terms(first)
    got_a = exchange(terms_a)
    far = each(flip_grid, after(own, terms_a), 2)
    own_dp = each(flip_dp, own)

    terms_1 = partial_terms(near)
    got_1 = exchange(terms_1)
    near_dp = each(flip_dp, near)
    corner = each(flip_grid, far, 1)
    far_dp = each(flip_dp, far)
    terms_3 = partial_terms(after(corner, terms_1))
    got_3 = exchange(terms_3)
    corner_dp = each(flip_dp, corner)
    terms_2 = partial_terms(after(far, terms_3))
    got_2 = exchange(terms_2)
    terms_b = partial_terms(after(last, terms_2))
    got_b = exchange(terms_b[:2])
    got_c = exchange(terms_b[2:])

    parts_a, held = finish(terms_a, got_a, first, each(lambda x: x[:half], own_dp), None)
    parts_1, held = finish(terms_1, got_1, near, near_dp, held)
    from_near = flip_grid(to_bf16(parts_1), 1)
    parts_3, held = finish(terms_3, got_3, corner, corner_dp, held)
    from_side = flip_grid(to_bf16(parts_3), 1)
    parts_2, held = finish(terms_2, got_2, far, far_dp, held)
    from_far = flip_grid(to_bf16(parts_2 + from_side.astype(jnp.float32)), 2)

    last_dp = each(lambda x: x[half:], own_dp)
    gate_pre, up_proj = summed(terms_b[:2], got_b)
    hidden = hidden_of(gate_pre, up_proj)
    hidden_dp = flip_dp(hidden)
    out_b = out_product(hidden)
    down_grad = grad_term(
        ordered(hidden, hidden_dp), ordered(last[1], last_dp[1]), held[2]
    )
    left = ordered(last[0], last_dp[0])
    (hidden_grad,) = summed(terms_b[2:], got_c)
    sums_again = summed(lax.optimization_barrier(terms_b[:2] + (hidden,))[:2], after(got_b, hidden))
    backs = backs_of(*sums_again, hidden_grad)
    backs_dp = each(flip_dp, backs)
    input_b = input_product(backs)
    gate_grad = grad_term(left, ordered(backs[0], backs_dp[0]), held[0])
    up_grad = grad_term(left, ordered(backs[1], backs_dp[1]), held[1])

    from_far = after(from_far, input_b)
    others = from_near.astype(jnp.float32) + from_far.astype(jnp.float32)
    block_out = to_bf16(
        own_acts.astype(jnp.float32) + (jnp.concatenate([parts_a[0], out_b]) + others[0])
    )
    input_grad = to_bf16(
        own_grads.astype(jnp.float32) + (jnp.concatenate([parts_a[1], input_b]) + others[1])
    )
    return (
        block_out[None, None],
        input_grad[None, None],
        gate_grad[None],
        up_grad[None],
        down_grad[None],
    )


def solution(mesh):
    plan = two_row_device if mesh.shape["grid"] == 8 and mesh.shape["dp"] == 2 else per_device
    return jax.shard_map(
        plan,
        mesh=mesh,
        in_specs=(
            P(("groups", "dp"), "grid", None, None),
            P(("groups", "dp"), "grid", None, None),
            P("grid", None, None),
            P("grid", None, None),
            P("grid", None, None),
        ),
        out_specs=(
            P(("groups", "dp"), "grid", None, None),
            P(("groups", "dp"), "grid", None, None),
            P(("groups", "grid"), None, None),
            P(("groups", "grid"), None, None),
            P(("groups", "grid"), None, None),
        ),
        check_vma=False,
    )
```

```python
import jax
import jax.numpy as jnp
from jax import lax
from jax.sharding import PartitionSpec as P


def from_partner(block, axis, stride):
    count = lax.axis_size(axis)
    route = []
    for low in range(count):
        high = low | 1 << stride
        if high != low and high < count:
            route += [(low, high), (high, low)]
    return lax.ppermute(block, axis, route)


def contract_rows(left, right):
    return lax.dot_general(
        left, right, (((0,), (0,)), ((), ())), preferred_element_type=jnp.float32
    )


def contract_cols(left, right):
    return lax.dot_general(
        left, right, (((1,), (1,)), ((), ())), preferred_element_type=jnp.float32
    )


def order_pair(is_upper, mine, other):
    return jnp.where(is_upper, jnp.concatenate([other, mine], 1), jnp.concatenate([mine, other], 1))


def column_sum(partial_term, total_rows, col_bits, row_bits, my_row):
    result_sum = partial_term(0, total_rows)
    for level_bit in range(row_bits - 1, -1, -1):
        half_rows = result_sum.shape[1] // 2
        lower_half = result_sum[:, :half_rows]
        upper_half = result_sum[:, half_rows:]
        is_upper = my_row >> level_bit & 1 == 1
        kept_half = jnp.where(is_upper, upper_half, lower_half)
        given_half = jnp.where(is_upper, lower_half, upper_half)
        result_sum = kept_half + from_partner(
            given_half.astype(jnp.bfloat16), "grid", col_bits + level_bit
        ).astype(given_half.dtype)
    return result_sum


def column_gather(pieces, col_bits, row_bits, my_row):
    for level_bit in range(row_bits):
        partner = from_partner(pieces, "grid", col_bits + level_bit)
        pieces = order_pair(my_row >> level_bit & 1 == 1, pieces, partner)
    return pieces


def row_sum(full_sum, col_bits, my_col):
    for level_bit in range(col_bits - 1, -1, -1):
        half_rows = full_sum.shape[0] // 2
        lower_half = full_sum[:half_rows]
        upper_half = full_sum[half_rows:]
        is_upper = my_col >> level_bit & 1 == 1
        kept_half = jnp.where(is_upper, upper_half, lower_half)
        given_half = jnp.where(is_upper, lower_half, upper_half)
        full_sum = kept_half + from_partner(
            given_half.astype(jnp.bfloat16), "grid", level_bit
        ).astype(given_half.dtype)
    return full_sum


def per_device(acts, cotangent, w_gate, w_up, w_down):
    grid_size = lax.axis_size("grid")
    grid_cols = min(8, grid_size // 2)
    grid_rows = grid_size // grid_cols
    col_bits = grid_cols.bit_length() - 1
    row_bits = grid_rows.bit_length() - 1
    position = lax.axis_index("grid")
    my_row = position // grid_cols
    my_col = position % grid_cols
    own_acts = acts[0, 0]
    own_grads = cotangent[0, 0]
    gate_tile = w_gate[0]
    up_tile = w_up[0]
    down_tile = w_down[0]
    gathered = jnp.stack([own_acts, own_grads])
    for level_bit in range(col_bits):
        partner = from_partner(gathered, "grid", level_bit)
        gathered = order_pair(my_col >> level_bit & 1 == 1, gathered, partner)
    inputs_row = gathered[0]
    out_grad_row = gathered[1]
    total_rows = inputs_row.shape[0]

    def gate_up_term(row_start, row_count):
        return jnp.stack(
            [
                jnp.dot(inputs_row, gate_tile, preferred_element_type=jnp.float32),
                jnp.dot(inputs_row, up_tile, preferred_element_type=jnp.float32),
            ]
        )

    summed = column_sum(gate_up_term, total_rows, col_bits, row_bits, my_row)
    gate_pre = summed[0]
    up_proj = summed[1]
    sigmoid_g = jax.nn.sigmoid(gate_pre)
    activated = gate_pre * sigmoid_g
    hidden = (activated * up_proj).astype(jnp.bfloat16)
    hidden_full = column_gather(hidden[None], col_bits, row_bits, my_row)[0]
    output_sum = row_sum(
        jnp.dot(hidden_full, down_tile, preferred_element_type=jnp.float32), col_bits, my_col
    )
    block_out = (own_acts.astype(jnp.float32) + output_sum).astype(jnp.bfloat16)

    def hidden_grad_term(row_start, row_count):
        return contract_cols(out_grad_row, down_tile)[None]

    hidden_grad = column_sum(hidden_grad_term, total_rows, col_bits, row_bits, my_row)[0]
    gate_back = (hidden_grad * up_proj * sigmoid_g * (1.0 + gate_pre * (1.0 - sigmoid_g))).astype(
        jnp.bfloat16
    )
    up_back = (hidden_grad * activated).astype(jnp.bfloat16)
    backs_full = column_gather(jnp.stack([gate_back, up_back]), col_bits, row_bits, my_row)
    down_local = contract_rows(hidden_full, out_grad_row)
    input_part = contract_cols(backs_full[0], gate_tile) + contract_cols(backs_full[1], up_tile)
    input_sum = row_sum(input_part, col_bits, my_col)
    input_grad = (own_grads.astype(jnp.float32) + input_sum).astype(jnp.bfloat16)
    gate_local = contract_rows(inputs_row, backs_full[0])
    up_local = contract_rows(inputs_row, backs_full[1])
    gate_total, up_total, down_total = (
        lax.psum(gate_local.astype(jnp.bfloat16), "dp").astype(jnp.float32),
        lax.psum(up_local.astype(jnp.bfloat16), "dp").astype(jnp.float32),
        lax.psum(down_local.astype(jnp.bfloat16), "dp").astype(jnp.float32),
    )
    return (
        block_out[None, None],
        input_grad[None, None],
        gate_total.astype(jnp.bfloat16)[None],
        up_total.astype(jnp.bfloat16)[None],
        down_total.astype(jnp.bfloat16)[None],
    )


def flip_grid(block, mask):
    count = lax.axis_size("grid")
    return lax.ppermute(block, "grid", [(i, i ^ mask) for i in range(count)])


def flip_dp(block):
    return lax.ppermute(block, "dp", [(0, 1), (1, 0)])


def after(value, *others):
    return lax.optimization_barrier((value,) + others)[0]


def two_row_device(acts, cotangent, w_gate, w_up, w_down):
    return two_row_body(acts[0, 0], cotangent[0, 0], w_gate[0], w_up[0], w_down[0])


def two_row_body(own_acts, own_grads, gate_tile, up_tile, down_tile):
    half = own_acts.shape[0] // 2
    is_upper = lax.axis_index("dp") == 1
    across = 4

    def each(move, pair, *mask):
        return tuple(move(x, *mask) for x in pair)

    def to_bf16(value):
        return value.astype(jnp.bfloat16)

    def partial_terms(pair):
        return (
            to_bf16(jnp.dot(pair[0], gate_tile, preferred_element_type=jnp.float32)),
            to_bf16(jnp.dot(pair[0], up_tile, preferred_element_type=jnp.float32)),
            to_bf16(contract_cols(pair[1], down_tile)),
        )

    def exchange(terms):
        return flip_grid(jnp.stack(terms), across)

    def summed(mine, other):
        return [m.astype(jnp.float32) + other[i].astype(jnp.float32) for i, m in enumerate(mine)]

    def gate_values(gate_pre):
        sigmoid_g = jax.nn.sigmoid(gate_pre)
        return sigmoid_g, gate_pre * sigmoid_g

    def hidden_of(gate_pre, up_proj):
        return to_bf16(gate_values(gate_pre)[1] * up_proj)

    def backs_of(gate_pre, up_proj, hidden_grad):
        sigmoid_g, activated = gate_values(gate_pre)
        gate_back = hidden_grad * up_proj * sigmoid_g * (1.0 + gate_pre * (1.0 - sigmoid_g))
        return to_bf16(gate_back), to_bf16(hidden_grad * activated)

    def out_product(hidden):
        return jnp.dot(hidden, down_tile, preferred_element_type=jnp.float32)

    def input_product(backs):
        return contract_cols(backs[0], gate_tile) + contract_cols(backs[1], up_tile)

    def ordered(*both):
        rows = []
        for mine, other in both:
            rows += [jnp.where(is_upper, other, mine), jnp.where(is_upper, mine, other)]
        return jnp.concatenate(rows)

    def grad_term(left, right, held):
        term = contract_rows(left, right)
        if held is not None:
            term = term + held.astype(jnp.float32)
        return to_bf16(term)

    def finish(mine, other):
        values = summed(mine, other)
        hidden = hidden_of(values[0], values[1])
        backs = backs_of(*values)
        units = jnp.stack((hidden,) + backs)
        units_dp = flip_dp(units)
        parts = jnp.stack([out_product(hidden), input_product(backs)])
        return parts, [(units[i], units_dp[i]) for i in range(3)]

    def weight_grads(pieces, held):
        left = ordered(*((pair[0], pair_dp[0]) for pair, pair_dp, _ in pieces))
        right = ordered(*((pair[1], pair_dp[1]) for pair, pair_dp, _ in pieces))
        units = [ordered(*(piece[2][i] for piece in pieces)) for i in range(3)]
        grads = (
            grad_term(left, units[1], held[0]),
            grad_term(left, units[2], held[1]),
            grad_term(units[0], right, held[2]),
        )
        return lax.optimization_barrier(grads)

    own = (own_acts, own_grads)
    near = each(flip_grid, own, 1)
    first = (own_acts[:half], own_grads[:half])
    last = (own_acts[half:], own_grads[half:])
    terms_a = partial_terms(first)
    got_a = exchange(terms_a)
    far = each(flip_grid, after(own, terms_a), 2)
    own_dp = each(flip_dp, own)

    terms_1 = partial_terms(near)
    got_1 = exchange(terms_1)
    near_dp = each(flip_dp, near)
    corner = each(flip_grid, far, 1)
    far_dp = each(flip_dp, far)
    terms_3 = partial_terms(after(corner, terms_1))
    got_3 = exchange(terms_3)
    corner_dp = each(flip_dp, corner)
    terms_2 = partial_terms(after(far, terms_3))
    got_2 = exchange(terms_2)
    terms_b = partial_terms(after(last, terms_2))
    got_b = exchange(terms_b[:2])
    got_c = exchange(terms_b[2:])

    first_dp = each(lambda x: x[:half], own_dp)
    parts_a, units_a = finish(terms_a, got_a)
    parts_1, units_1 = finish(terms_1, got_1)
    from_near = flip_grid(to_bf16(parts_1), 1)
    held = weight_grads(((first, first_dp, units_a), (near, near_dp, units_1)), (None, None, None))
    parts_3, units_3 = finish(terms_3, got_3)
    from_side = flip_grid(to_bf16(parts_3), 1)
    held = weight_grads(((corner, corner_dp, units_3),), held)
    parts_2, units_2 = finish(terms_2, got_2)
    from_far = flip_grid(to_bf16(parts_2 + from_side.astype(jnp.float32)), 2)

    last_dp = each(lambda x: x[half:], own_dp)
    gate_pre, up_proj = summed(terms_b[:2], got_b)
    hidden = hidden_of(gate_pre, up_proj)
    hidden_dp = flip_dp(hidden)
    out_b = out_product(hidden)
    down_grad = grad_term(
        ordered(units_2[0], (hidden, hidden_dp)),
        ordered((far[1], far_dp[1]), (last[1], last_dp[1])),
        held[2],
    )
    left = ordered((far[0], far_dp[0]), (last[0], last_dp[0]))
    (hidden_grad,) = summed(terms_b[2:], got_c)
    sums_again = summed(lax.optimization_barrier(terms_b[:2] + (hidden,))[:2], after(got_b, hidden))
    backs = backs_of(*sums_again, hidden_grad)
    backs_dp = each(flip_dp, backs)
    input_b = input_product(backs)
    gate_grad = grad_term(left, ordered(units_2[1], (backs[0], backs_dp[0])), held[0])
    up_grad = grad_term(left, ordered(units_2[2], (backs[1], backs_dp[1])), held[1])

    from_far = after(from_far, input_b)
    others = from_near.astype(jnp.float32) + from_far.astype(jnp.float32)
    block_out = to_bf16(
        own_acts.astype(jnp.float32) + (jnp.concatenate([parts_a[0], out_b]) + others[0])
    )
    input_grad = to_bf16(
        own_grads.astype(jnp.float32) + (jnp.concatenate([parts_a[1], input_b]) + others[1])
    )
    return (
        block_out[None, None],
        input_grad[None, None],
        gate_grad[None],
        up_grad[None],
        down_grad[None],
    )


def solution(mesh):
    plan = two_row_device if mesh.shape["grid"] == 8 and mesh.shape["dp"] == 2 else per_device
    step = jax.shard_map(
        plan,
        mesh=mesh,
        in_specs=(
            P(("groups", "dp"), "grid", None, None),
            P(("groups", "dp"), "grid", None, None),
            P("grid", None, None),
            P("grid", None, None),
            P("grid", None, None),
        ),
        out_specs=(
            P(("groups", "dp"), "grid", None, None),
            P(("groups", "dp"), "grid", None, None),
            P(("groups", "grid"), None, None),
            P(("groups", "grid"), None, None),
            P(("groups", "grid"), None, None),
        ),
        check_vma=False,
    )
    if plan is per_device:
        return step
    return step
```
